32 devices in a mesh: seq: 8 (over y, x, core), dp: 4 (over z).
Axes of the slice: x: 2, y: 2, z: 4, core: 2. Of those that a mesh axis runs over, the one named last changes fastest.
Arguments:
- query: bfloat16 [4, 1536, 1280], P('dp', 'seq'), may hold values from -52 to 52, as said below
- keys: bfloat16 [4, 1536, 1280], P('dp', 'seq'), may hold values from -6 to 6, as said below
- values: bfloat16 [4, 1536, 1280], P('dp', 'seq'), may hold values from -6 to 6
- attn: bfloat16 [4, 1536, 1280], P('dp', 'seq'), may hold values from -6 to 6
- d_block: bfloat16 [4, 1536, 1280], P('dp', 'seq'), may hold values from -6 to 6
- w_out: bfloat16 [1280, 1280], P('dp'), may hold values from -0.15625 to 0.15625
Outputs:
- d_query: bfloat16 [4, 1536, 1280], P('dp', 'seq')
- d_keys: bfloat16 [4, 1536, 1280], P('dp', 'seq')
- d_values: bfloat16 [4, 1536, 1280], P('dp', 'seq')
- d_weight: float32 [1280, 1280], P('dp')
The draws below stay inside these ranges and needn't reach their ends.
Inputs may be any that keep to these rules, and one draw needn't show every extreme that they name: Some query patches may lie along the sum of two keys of the same video. keys has entries of order one.
All inputs are finite; a program needn't handle non-finite values.
Results may differ from the reference program's by a relative error of at most 0.0058.
Values may be sent and summed in bfloat16 or wider, within the bound.
A program may use at most 64 MiB of HBM per device.

```python
import jax
import jax.numpy as jnp
from jax import lax

HEADS = 16
HEAD_DIM = 80
D = 1280
PATCHES = 1536
VIDEOS = 4


def shared_pair(key):
    shape_all = (VIDEOS, PATCHES, HEADS * HEAD_DIM)
    keys_raw = jnp.clip(jax.random.normal(jax.random.fold_in(key, 101), shape_all, jnp.float32), -6.0, 6.0)
    query_raw = jnp.clip(jax.random.normal(jax.random.fold_in(key, 202), shape_all, jnp.float32), -6.0, 6.0)
    keys_out = keys_raw
    query_out = query_raw
    return (query_out, keys_out)


def draw_query(key, part):
    return shared_pair(key)[0].astype(jnp.bfloat16)


def draw_keys(key, part):
    return shared_pair(key)[1].astype(jnp.bfloat16)


def raised(entries, own_key, source, target, parts, factor):
    owner, partner = [(jnp.arange(entries.shape[axis_at]) // (entries.shape[axis_at] // parts)).reshape([-1 if axis == axis_at else 1 for axis in range(entries.ndim)]) for axis_at in (source, target)]
    chosen = jax.random.permutation(own_key, parts)[partner]
    strong = (owner == chosen) | (owner == (partner + parts // 2) % parts)
    return jnp.where(strong, factor * entries, entries)


def block_scale(rng, shape, shards, low, top_value):
    gain, own = 1.0, jax.random.fold_in(rng, 6)
    for position, shards_of in shards:
        steps = jnp.exp(jax.random.uniform(jax.random.fold_in(own, position), (shards_of,), jnp.float32, low / len(shards), top_value / len(shards)))
        gain = gain * jnp.repeat(steps, shape[position] // shards_of).reshape([-1 if axis == position else 1 for axis in range(len(shape))])
    return gain


def noise(key, shape, deviation, limit, shards=(), kind=jnp.bfloat16):
    values = deviation * jax.random.normal(key, shape, jnp.float32)
    if shards:
        values = values * block_scale(key, shape, shards, -0.22, 0.18)
    return jnp.clip(values, -limit, limit).astype(kind)


def noise_with(rng, extent, width, reach, shards, heavy, held_as=jnp.bfloat16):
    drawn = width * jax.random.normal(rng, extent, jnp.float32)
    if shards:
        drawn = drawn * block_scale(rng, extent, shards, -0.22, 0.18)
    return jnp.clip(raised(drawn, jax.random.fold_in(rng, 3), *heavy), -reach, reach).astype(held_as)


def setup_inputs(seed: int = 0) -> dict:
    seeds = jax.random.split(jax.random.key(seed), 7)
    query = draw_query(jax.random.fold_in(seeds[6], 71), 0)
    keys = draw_keys(jax.random.fold_in(seeds[6], 71), 0)
    values = noise(seeds[2], (VIDEOS, PATCHES, D), 1.0, 6.0, ((0, 4), (1, 8)))
    attn = noise_with(seeds[3], (VIDEOS, PATCHES, D), 1.0, 6.0, ((0, 4), (1, 8)), (1, 2, 8, 2.0))
    d_block = noise(seeds[4], (VIDEOS, PATCHES, D), 1.0, 6.0, ((0, 4), (1, 8)))
    w_out = noise(seeds[5], (D, D), D ** -0.5, 0.15625, ((0, 4),))
    return dict(query=query, keys=keys, values=values, attn=attn, d_block=d_block, w_out=w_out)


def head_gradients(item):
    query_h, keys_h, values_h, dout_h, delta_h = item
    score_scale = HEAD_DIM ** -0.5
    scores = jnp.dot(query_h, keys_h.T, preferred_element_type=jnp.float32) * score_scale
    row_max = jnp.max(scores, axis=1, keepdims=True)
    lse = row_max + jnp.log(jnp.sum(jnp.exp(scores - row_max), axis=1, keepdims=True))
    probs = jnp.exp(scores - lse)
    probs_low = probs.astype(jnp.bfloat16)
    d_values = jnp.dot(probs_low.T, dout_h, preferred_element_type=jnp.float32)
    d_probs = jnp.dot(dout_h, values_h.T, preferred_element_type=jnp.float32)
    d_scores = (score_scale * probs * (d_probs - delta_h[:, None])).astype(jnp.bfloat16)
    d_query = jnp.dot(d_scores, keys_h, preferred_element_type=jnp.float32)
    d_keys = jnp.dot(d_scores.T, query_h, preferred_element_type=jnp.float32)
    return (d_query.astype(jnp.bfloat16), d_keys.astype(jnp.bfloat16), d_values.astype(jnp.bfloat16))


def reference(query, keys, values, attn, d_block, w_out):
    features = HEADS * HEAD_DIM
    grad_y = d_block.reshape(VIDEOS * PATCHES, features)
    attn_rows = attn.reshape(VIDEOS * PATCHES, features)
    d_out = jnp.dot(grad_y, w_out.T, preferred_element_type=jnp.float32).astype(jnp.bfloat16)
    delta = jnp.sum((d_out.astype(jnp.float32) * attn_rows.astype(jnp.float32)).reshape(VIDEOS, PATCHES, HEADS, HEAD_DIM), axis=3)

    def by_head(array):
        return array.reshape(VIDEOS, PATCHES, HEADS, HEAD_DIM).transpose(0, 2, 1, 3).reshape(VIDEOS * HEADS, PATCHES, HEAD_DIM)

    delta_heads = delta.transpose(0, 2, 1).reshape(VIDEOS * HEADS, PATCHES)
    d_query, d_keys, d_values = lax.map(head_gradients, (by_head(query), by_head(keys), by_head(values), by_head(d_out.reshape(VIDEOS, PATCHES, features)), delta_heads))

    def by_patch(array):
        return array.reshape(VIDEOS, HEADS, PATCHES, HEAD_DIM).transpose(0, 2, 1, 3).reshape(VIDEOS, PATCHES, features)

    total = jnp.dot(attn_rows.T, grad_y, preferred_element_type=jnp.float32)
    d_weight = total * (1.0 / (float(VIDEOS * PATCHES) ** 0.5))
    return (by_patch(d_query), by_patch(d_keys), by_patch(d_values), d_weight)
```

```python
import functools
import math

import jax
import jax.numpy as jnp
from jax import lax
from jax.experimental import pallas as pl
from jax.experimental.pallas import tpu as pltpu
from jax.sharding import PartitionSpec as P

HEAD_DIM = 80
MESH = pl.DeviceIdType.MESH
VMEM_LIMIT = 60 * 1024 * 1024
LAST = (((1,), (1,)), ((), ()))
FIRST = (((0,), (0,)), ((), ()))


def gather_kernel(
    seq, dp, q_ref, k_ref, v_ref, a_ref, g_ref, w_ref, pack_out, g_out, w_out,
    packed, g_send, g_recv, f_send, w_send, w_recv, p_send, p_recv, local_sem,
):
    s = lax.axis_index("seq")
    d = lax.axis_index("dp")
    ratio = seq // dp
    home = s // ratio
    partner = s + 1 - 2 * (s % 2)
    width = k_ref.shape[1] // seq

    barrier = pltpu.get_barrier_semaphore()
    for step in range(1, seq):
        pl.semaphore_signal(barrier, inc=1, device_id=(lax.rem(s + step, seq), d), device_id_type=MESH)
    for step in range(1, dp):
        pl.semaphore_signal(barrier, inc=1, device_id=(s, lax.rem(d + step, dp)), device_id_type=MESH)
    pl.semaphore_wait(barrier, seq + dp - 2)

    def w_copy(step):
        return pltpu.make_async_remote_copy(
            src_ref=w_ref.at[s % ratio],
            dst_ref=w_out,
            send_sem=w_send.at[step],
            recv_sem=w_recv,
            device_id=(s, lax.rem(d + step, dp)),
            device_id_type=MESH,
        )

    def direct(step):
        return pltpu.make_async_remote_copy(
            src_ref=g_ref,
            dst_ref=g_out.at[s],
            send_sem=g_send.at[step],
            recv_sem=g_recv.at[s],
            device_id=(lax.rem(s + 2 * step, seq), d),
            device_id_type=MESH,
        )

    def forward(step):
        source = lax.rem(s + seq - 2 * step, seq)
        return pltpu.make_async_remote_copy(
            src_ref=g_ref if step == 0 else g_out.at[source],
            dst_ref=g_out.at[source],
            send_sem=f_send.at[step],
            recv_sem=g_recv.at[source],
            device_id=(partner, d),
            device_id_type=MESH,
        )

    def arrived(source):
        pltpu.make_async_remote_copy(
            src_ref=g_ref,
            dst_ref=g_out.at[source],
            send_sem=f_send.at[0],
            recv_sem=g_recv.at[source],
            device_id=(partner, d),
            device_id_type=MESH,
        ).wait_recv()

    def pack_copy(step):
        peer = lax.rem(s + step, seq)
        return pltpu.make_async_remote_copy(
            src_ref=packed.at[peer],
            dst_ref=pack_out.at[s],
            send_sem=p_send.at[step],
            recv_sem=p_recv.at[s],
            device_id=(peer, d),
            device_id_type=MESH,
        )

    own_g = pltpu.make_async_copy(g_ref, g_out.at[s], local_sem.at[0])
    own_w = pltpu.make_async_copy(w_ref.at[s % ratio], w_out, local_sem.at[1])
    own_pack = pltpu.make_async_copy(packed.at[s], pack_out.at[s], local_sem.at[2])

    for step in range(1, seq // 2):
        direct(step).start()
    forward(0).start()
    own_g.start()

    @pl.when(home == d)
    def _():
        for step in range(1, dp):
            w_copy(step).start()
        own_w.start()

    for peer in range(seq):
        for index, ref in enumerate((q_ref, k_ref, v_ref, a_ref)):
            packed[peer, :, index * width : (index + 1) * width] = ref[
                :, peer * width : (peer + 1) * width
            ]
    for step in range(1, seq):
        pack_copy(step).start()
    own_pack.start()

    for step in range(1, seq // 2):
        arrived(lax.rem(s + seq - 2 * step, seq))
        forward(step).start()
    for step in range(seq // 2):
        arrived(lax.rem(partner + seq - 2 * step, seq))
    for step in range(1, seq):
        source = lax.rem(s + seq - step, seq)
        pltpu.make_async_remote_copy(
            src_ref=packed.at[source],
            dst_ref=pack_out.at[source],
            send_sem=p_send.at[step],
            recv_sem=p_recv.at[source],
            device_id=(source, d),
            device_id_type=MESH,
        ).wait_recv()

    @pl.when(home == d)
    def _():
        for step in range(1, dp):
            w_copy(step).wait_send()
        own_w.wait()

    @pl.when(home != d)
    def _():
        w_copy(1).wait_recv()

    own_g.wait()
    own_pack.wait()
    for step in range(1, seq // 2):
        direct(step).wait_send()
    for step in range(seq // 2):
        forward(step).wait_send()
    for step in range(1, seq):
        pack_copy(step).wait_send()


def gather(seq, dp, query, keys, values, attn, grad_y, w_rows):
    rows, features = query.shape
    width = features // seq
    dma = pltpu.SemaphoreType.DMA
    vmem = pl.BlockSpec(memory_space=pltpu.VMEM)
    hbm = pl.BlockSpec(memory_space=pl.ANY)
    return pl.pallas_call(
        functools.partial(gather_kernel, seq, dp),
        out_shape=(
            jax.ShapeDtypeStruct((seq, rows, 4 * width), jnp.bfloat16),
            jax.ShapeDtypeStruct((seq, rows, features), jnp.bfloat16),
            jax.ShapeDtypeStruct((width, features), jnp.bfloat16),
        ),
        in_specs=[vmem] * 6,
        out_specs=(hbm, hbm, hbm),
        scratch_shapes=[
            pltpu.VMEM((seq, rows, 4 * width), jnp.bfloat16),
            dma((seq,)),
            dma((seq,)),
            dma((seq,)),
            dma((dp,)),
            dma(()),
            dma((seq,)),
            dma((seq,)),
            dma((3,)),
        ],
        compiler_params=pltpu.CompilerParams(
            collective_id=0, has_side_effects=True, vmem_limit_bytes=VMEM_LIMIT
        ),
        name="gather_heads",
    )(query, keys, values, attn, grad_y, w_rows)


def attention_kernel(
    heads, block_rows, factor, pack_ref, g_ref, w_ref, out_ref, dw_ref,
    q_s, k_s, v_s, do_s, delta_s, dk_s, dv_s,
):
    total = pack_ref.shape[0]
    width = heads * HEAD_DIM
    scale = HEAD_DIM ** (-0.5)
    to_log2 = scale * math.log2(math.e)

    @pl.loop(0, total // block_rows)
    def _(block):
        rows = pl.ds(pl.multiple_of(block * block_rows, block_rows), block_rows)
        d_out = lax.dot_general(
            g_ref[rows, :], w_ref[...], LAST, preferred_element_type=jnp.float32
        ).astype(jnp.bfloat16)
        for h in range(heads):
            low = h * HEAD_DIM
            q_s[h, rows, :] = pack_ref[rows, low : low + HEAD_DIM]
            k_s[h, rows, :] = pack_ref[rows, width + low : width + low + HEAD_DIM]
            v_s[h, rows, :] = pack_ref[rows, 2 * width + low : 2 * width + low + HEAD_DIM]
            a_h = pack_ref[rows, 3 * width + low : 3 * width + low + HEAD_DIM]
            do_h = d_out[:, low : low + HEAD_DIM]
            do_s[h, rows, :] = do_h
            product = do_h.astype(jnp.float32) * a_h.astype(jnp.float32)
            delta_s[h, block] = jnp.sum(product.T, axis=0, keepdims=True)

    pieces = dw_ref.shape[0]
    piece = dw_ref.shape[1]
    d_weight = lax.dot_general(
        pack_ref[:, 3 * width : 4 * width], g_ref[...], FIRST, preferred_element_type=jnp.float32
    )
    for index in range(pieces):
        dw_ref[index] = (d_weight[index * piece : (index + 1) * piece, :] * factor).astype(
            jnp.bfloat16
        )

    dk_s[...] = jnp.zeros_like(dk_s)
    dv_s[...] = jnp.zeros_like(dv_s)

    @pl.loop(0, total // block_rows)
    def _(block):
        rows = pl.ds(pl.multiple_of(block * block_rows, block_rows), block_rows)
        for h in range(heads):
            q_b = q_s[h, rows, :]
            do_b = do_s[h, rows, :]
            keys = k_s[h]
            scores = lax.dot_general(keys, q_b, LAST, preferred_element_type=jnp.float32)
            top = jnp.max(scores, axis=0, keepdims=True)
            exps = jnp.exp2((scores - top) * to_log2)
            probs = exps * (1.0 / jnp.sum(exps, axis=0, keepdims=True))
            d_probs = lax.dot_general(v_s[h], do_b, LAST, preferred_element_type=jnp.float32)
            d_scores = (probs * (d_probs - delta_s[h, block]) * scale).astype(jnp.bfloat16)
            dv_s[h] += jnp.dot(probs.astype(jnp.bfloat16), do_b, preferred_element_type=jnp.float32)
            dk_s[h] += jnp.dot(d_scores, q_b, preferred_element_type=jnp.float32)
            dq_t = lax.dot_general(keys, d_scores, FIRST, preferred_element_type=jnp.float32)
            out_ref[rows, h * HEAD_DIM : (h + 1) * HEAD_DIM] = dq_t.T.astype(jnp.bfloat16)

    for h in range(heads):
        low = h * HEAD_DIM
        out_ref[:, width + low : width + low + HEAD_DIM] = dk_s[h].astype(jnp.bfloat16)
        out_ref[:, 2 * width + low : 2 * width + low + HEAD_DIM] = dv_s[h].astype(jnp.bfloat16)


def attention(seq, factor, packed, grad_y, w_rows):
    total = packed.shape[0]
    width, features = w_rows.shape
    heads = width // HEAD_DIM
    block_rows = 512
    while total % block_rows:
        block_rows //= 2
    vmem = pl.BlockSpec(memory_space=pltpu.VMEM)
    low = pltpu.VMEM((heads, total, HEAD_DIM), jnp.bfloat16)
    wide = pltpu.VMEM((heads, total, HEAD_DIM), jnp.float32)
    return pl.pallas_call(
        functools.partial(attention_kernel, heads, block_rows, factor),
        out_shape=(
            jax.ShapeDtypeStruct((total, 3 * width), jnp.bfloat16),
            jax.ShapeDtypeStruct((seq, width // seq, features), jnp.bfloat16),
        ),
        in_specs=[vmem] * 3,
        out_specs=(vmem, vmem),
        scratch_shapes=[
            low, low, low, low,
            pltpu.VMEM((heads, total // block_rows, 1, block_rows), jnp.float32),
            wide, wide,
        ],
        compiler_params=pltpu.CompilerParams(vmem_limit_bytes=VMEM_LIMIT),
        name="attention_backward",
    )(packed, grad_y, w_rows)


def scatter_kernel(
    seq, dp, grad_ref, dw_ref, dq_ref, dk_ref, dv_ref, out_ref,
    landed, parts, total, spread, p_send, p_recv, w_send, w_recv, t_send, t_recv, local_sem,
):
    s = lax.axis_index("seq")
    d = lax.axis_index("dp")
    ratio = seq // dp
    home = s // ratio
    slot = d * ratio + s % ratio
    width = dq_ref.shape[1] // seq
    piece = dw_ref.shape[1]

    barrier = pltpu.get_barrier_semaphore()
    for step in range(1, seq):
        pl.semaphore_signal(barrier, inc=1, device_id=(lax.rem(s + step, seq), d), device_id_type=MESH)
    for row in range(dp):
        for column in range(ratio):
            @pl.when(jnp.logical_or(row != d, d * ratio + column != s))
            def _():
                pl.semaphore_signal(
                    barrier, inc=1, device_id=(d * ratio + column, row), device_id_type=MESH
                )

    @pl.when(home == d)
    def _():
        pl.semaphore_wait(barrier, 2 * seq - 2)

    @pl.when(home != d)
    def _():
        pl.semaphore_wait(barrier, 2 * seq - 1)

    def w_copy(peer):
        return pltpu.make_async_remote_copy(
            src_ref=dw_ref.at[peer],
            dst_ref=parts.at[slot],
            send_sem=w_send.at[peer],
            recv_sem=w_recv.at[slot],
            device_id=(peer, home),
            device_id_type=MESH,
        )

    def grad_copy(step):
        peer = lax.rem(s + step, seq)
        return pltpu.make_async_remote_copy(
            src_ref=grad_ref.at[peer],
            dst_ref=landed.at[s],
            send_sem=p_send.at[step],
            recv_sem=p_recv.at[s],
            device_id=(peer, d),
            device_id_type=MESH,
        )

    def spread_copy(step):
        peer = lax.rem(s + step, seq)
        return pltpu.make_async_remote_copy(
            src_ref=total,
            dst_ref=spread.at[s],
            send_sem=t_send.at[step],
            recv_sem=t_recv.at[s],
            device_id=(peer, d),
            device_id_type=MESH,
        )

    own_part = pltpu.make_async_copy(dw_ref.at[s], parts.at[slot], local_sem.at[0])
    own_grad = pltpu.make_async_copy(grad_ref.at[s], landed.at[s], local_sem.at[1])
    for step in range(seq):
        peer = lax.rem(s + step, seq)

        @pl.when(jnp.logical_or(home != d, peer != s))
        def _():
            w_copy(peer).start()

    @pl.when(home == d)
    def _():
        own_part.start()

    for step in range(1, seq):
        grad_copy(step).start()
    own_grad.start()

    for row in range(dp):
        for column in range(ratio):
            source = row * ratio + column

            @pl.when(jnp.logical_or(row != d, d * ratio + column != s))
            def _():
                pltpu.make_async_remote_copy(
                    src_ref=dw_ref.at[0],
                    dst_ref=parts.at[source],
                    send_sem=w_send.at[0],
                    recv_sem=w_recv.at[source],
                    device_id=(d * ratio + column, row),
                    device_id_type=MESH,
                ).wait_recv()

    @pl.when(home == d)
    def _():
        own_part.wait()

    for column in range(ratio):
        value = parts[column].astype(jnp.float32)
        for row in range(1, dp):
            value = value + parts[row * ratio + column].astype(jnp.float32)
        total[column] = value.astype(jnp.bfloat16)
    for step in range(1, seq):
        spread_copy(step).start()
    own_total = pltpu.make_async_copy(total, spread.at[s], local_sem.at[2])
    own_total.start()

    own_grad.wait()
    for step in range(1, seq):
        source = lax.rem(s + seq - step, seq)
        pltpu.make_async_remote_copy(
            src_ref=grad_ref.at[source],
            dst_ref=landed.at[source],
            send_sem=p_send.at[step],
            recv_sem=p_recv.at[source],
            device_id=(source, d),
            device_id_type=MESH,
        ).wait_recv()
    for source in range(seq):
        for index, ref in enumerate((dq_ref, dk_ref, dv_ref)):
            ref[:, source * width : (source + 1) * width] = landed[
                source, :, index * width : (index + 1) * width
            ]

    own_total.wait()
    for step in range(1, seq):
        source = lax.rem(s + seq - step, seq)
        pltpu.make_async_remote_copy(
            src_ref=total,
            dst_ref=spread.at[source],
            send_sem=t_send.at[step],
            recv_sem=t_recv.at[source],
            device_id=(source, d),
            device_id_type=MESH,
        ).wait_recv()
    for source in range(seq):
        for column in range(ratio):
            start = column * width + source * piece
            out_ref[start : start + piece, :] = spread[source, column].astype(jnp.float32)

    for step in range(seq):
        peer = lax.rem(s + step, seq)

        @pl.when(jnp.logical_or(home != d, peer != s))
        def _():
            w_copy(peer).wait_send()

    for step in range(1, seq):
        grad_copy(step).wait_send()
        spread_copy(step).wait_send()


def scatter(seq, dp, grads, dw_parts):
    rows = grads.shape[1]
    piece, features = dw_parts.shape[1:]
    ratio = seq // dp
    dma = pltpu.SemaphoreType.DMA
    vmem = pl.BlockSpec(memory_space=pltpu.VMEM)
    block = jax.ShapeDtypeStruct((rows, features), jnp.bfloat16)
    return pl.pallas_call(
        functools.partial(scatter_kernel, seq, dp),
        out_shape=(
            block, block, block,
            jax.ShapeDtypeStruct((features // dp, features), jnp.float32),
        ),
        in_specs=[vmem] * 2,
        out_specs=(vmem,) * 4,
        scratch_shapes=[
            pltpu.VMEM(grads.shape, jnp.bfloat16),
            pltpu.VMEM((dp * ratio, piece, features), jnp.bfloat16),
            pltpu.VMEM((ratio, piece, features), jnp.bfloat16),
            pltpu.VMEM((seq, ratio, piece, features), jnp.bfloat16),
            dma((seq,)),
            dma((seq,)),
            dma((seq,)),
            dma((dp * ratio,)),
            dma((seq,)),
            dma((seq,)),
            dma((3,)),
        ],
        compiler_params=pltpu.CompilerParams(
            collective_id=1, has_side_effects=True, vmem_limit_bytes=VMEM_LIMIT
        ),
        name="scatter_gradients",
    )(grads, dw_parts)


def body(query, keys, values, attn, d_block, w_out):
    seq = lax.axis_size("seq")
    dp = lax.axis_size("dp")
    rows, features = query.shape[1:]
    width = features // seq
    flat = lambda array: array.reshape(rows, features)
    packed, grad_y, w_rows = gather(
        seq, dp, flat(query), flat(keys), flat(values), flat(attn), flat(d_block),
        w_out.reshape(seq // dp, width, features),
    )
    factor = 1.0 / float(dp * rows * seq) ** 0.5
    grads, dw_parts = attention(
        seq, factor,
        packed.reshape(seq * rows, 4 * width),
        grad_y.reshape(seq * rows, features),
        w_rows,
    )
    d_query, d_keys, d_values, d_weight = scatter(
        seq, dp, grads.reshape(seq, rows, 3 * width), dw_parts
    )
    whole = lambda array: array.reshape(1, rows, features)
    return whole(d_query), whole(d_keys), whole(d_values), d_weight


def solution(mesh):
    blocks = P("dp", "seq", None)
    return jax.shard_map(
        body,
        mesh=mesh,
        in_specs=(blocks,) * 5 + (P("dp", None),),
        out_specs=(blocks, blocks, blocks, P("dp", None)),
        check_vma=False,
    )
```

```python
import functools
import math

import jax
import jax.numpy as jnp
from jax import lax
from jax.experimental import pallas as pl
from jax.experimental.pallas import tpu as pltpu
from jax.sharding import PartitionSpec as P

HEAD_DIM = 80
MESH = pl.DeviceIdType.MESH
VMEM_LIMIT = 60 * 1024 * 1024
LAST = (((1,), (1,)), ((), ()))
FIRST = (((0,), (0,)), ((), ()))


def gather_kernel(
    seq, dp, q_ref, k_ref, v_ref, a_ref, g_ref, w_ref, pack_out, g_out, w_out,
    packed, g_send, g_recv, f_send, w_send, w_recv, p_send, p_recv, local_sem,
):
    s = lax.axis_index("seq")
    d = lax.axis_index("dp")
    ratio = seq // dp
    home = s // ratio
    partner = s + 1 - 2 * (s % 2)
    width = k_ref.shape[1] // seq

    barrier = pltpu.get_barrier_semaphore()
    for step in range(1, seq):
        pl.semaphore_signal(barrier, inc=1, device_id=(lax.rem(s + step, seq), d), device_id_type=MESH)
    for step in range(1, dp):
        pl.semaphore_signal(barrier, inc=1, device_id=(s, lax.rem(d + step, dp)), device_id_type=MESH)
    pl.semaphore_wait(barrier, seq + dp - 2)

    def w_copy(step):
        return pltpu.make_async_remote_copy(
            src_ref=w_ref.at[s % ratio],
            dst_ref=w_out,
            send_sem=w_send.at[step],
            recv_sem=w_recv,
            device_id=(s, lax.rem(d + step, dp)),
            device_id_type=MESH,
        )

    def direct(step):
        return pltpu.make_async_remote_copy(
            src_ref=g_ref,
            dst_ref=g_out.at[s],
            send_sem=g_send.at[step],
            recv_sem=g_recv.at[s],
            device_id=(lax.rem(s + 2 * step, seq), d),
            device_id_type=MESH,
        )

    def forward(step):
        source = lax.rem(s + seq - 2 * step, seq)
        return pltpu.make_async_remote_copy(
            src_ref=g_ref if step == 0 else g_out.at[source],
            dst_ref=g_out.at[source],
            send_sem=f_send.at[step],
            recv_sem=g_recv.at[source],
            device_id=(partner, d),
            device_id_type=MESH,
        )

    def arrived(source):
        pltpu.make_async_remote_copy(
            src_ref=g_ref,
            dst_ref=g_out.at[source],
            send_sem=f_send.at[0],
            recv_sem=g_recv.at[source],
            device_id=(partner, d),
            device_id_type=MESH,
        ).wait_recv()

    def pack_copy(step):
        peer = lax.rem(s + step, seq)
        return pltpu.make_async_remote_copy(
            src_ref=packed.at[peer],
            dst_ref=pack_out.at[s],
            send_sem=p_send.at[step],
            recv_sem=p_recv.at[s],
            device_id=(peer, d),
            device_id_type=MESH,
        )

    own_g = pltpu.make_async_copy(g_ref, g_out.at[s], local_sem.at[0])
    own_w = pltpu.make_async_copy(w_ref.at[s % ratio], w_out, local_sem.at[1])
    own_pack = pltpu.make_async_copy(packed.at[s], pack_out.at[s], local_sem.at[2])

    for step in range(1, seq // 2):
        direct(step).start()
    forward(0).start()
    own_g.start()

    @pl.when(home == d)
    def _():
        for step in range(1, dp):
            w_copy(step).start()
        own_w.start()

    for peer in range(seq):
        for index, ref in enumerate((q_ref, k_ref, v_ref, a_ref)):
            packed[peer, :, index * width : (index + 1) * width] = ref[
                :, peer * width : (peer + 1) * width
            ]
    for step in range(1, seq):
        pack_copy(step).start()
    own_pack.start()

    for step in range(1, seq // 2):
        arrived(lax.rem(s + seq - 2 * step, seq))
        forward(step).start()
    for step in range(seq // 2):
        arrived(lax.rem(partner + seq - 2 * step, seq))
    for step in range(1, seq):
        source = lax.rem(s + seq - step, seq)
        pltpu.make_async_remote_copy(
            src_ref=packed.at[source],
            dst_ref=pack_out.at[source],
            send_sem=p_send.at[step],
            recv_sem=p_recv.at[source],
            device_id=(source, d),
            device_id_type=MESH,
        ).wait_recv()

    @pl.when(home == d)
    def _():
        for step in range(1, dp):
            w_copy(step).wait_send()
        own_w.wait()

    @pl.when(home != d)
    def _():
        w_copy(1).wait_recv()

    own_g.wait()
    own_pack.wait()
    for step in range(1, seq // 2):
        direct(step).wait_send()
    for step in range(seq // 2):
        forward(step).wait_send()
    for step in range(1, seq):
        pack_copy(step).wait_send()


def gather(seq, dp, query, keys, values, attn, grad_y, w_rows):
    rows, features = query.shape
    width = features // seq
    dma = pltpu.SemaphoreType.DMA
    vmem = pl.BlockSpec(memory_space=pltpu.VMEM)
    hbm = pl.BlockSpec(memory_space=pl.ANY)
    return pl.pallas_call(
        functools.partial(gather_kernel, seq, dp),
        out_shape=(
            jax.ShapeDtypeStruct((seq, rows, 4 * width), jnp.bfloat16),
            jax.ShapeDtypeStruct((seq, rows, features), jnp.bfloat16),
            jax.ShapeDtypeStruct((width, features), jnp.bfloat16),
        ),
        in_specs=[vmem] * 6,
        out_specs=(hbm, hbm, hbm),
        scratch_shapes=[
            pltpu.VMEM((seq, rows, 4 * width), jnp.bfloat16),
            dma((seq,)),
            dma((seq,)),
            dma((seq,)),
            dma((dp,)),
            dma(()),
            dma((seq,)),
            dma((seq,)),
            dma((3,)),
        ],
        compiler_params=pltpu.CompilerParams(
            collective_id=0, has_side_effects=True, vmem_limit_bytes=VMEM_LIMIT
        ),
        name="gather_heads",
    )(query, keys, values, attn, grad_y, w_rows)


def backward_kernel(
    seq, dp, heads, block_rows, factor, pack_ref, g_ref, w_ref, landed, spread,
    q_s, k_s, v_s, do_s, delta_s, dk_s, dv_s, grad_s, dw_s, parts, total_s,
    p_send, p_recv, w_send, w_recv, t_send, f_send, t_recv, local_sem,
):
    s = lax.axis_index("seq")
    d = lax.axis_index("dp")
    ratio = seq // dp
    home = s // ratio
    slot = d * ratio + s % ratio
    partner = s + 1 - 2 * (s % 2)
    patches = pack_ref.shape[0]
    rows_here = patches // seq
    width = heads * HEAD_DIM
    scale = HEAD_DIM ** (-0.5)
    to_log2 = scale * math.log2(math.e)

    def w_copy(peer):
        return pltpu.make_async_remote_copy(
            src_ref=dw_s.at[peer],
            dst_ref=parts.at[slot],
            send_sem=w_send.at[peer],
            recv_sem=w_recv.at[slot],
            device_id=(peer, home),
            device_id_type=MESH,
        )

    def grad_copy(h, peer, source):
        start = pl.multiple_of(peer * rows_here, rows_here)
        return pltpu.make_async_remote_copy(
            src_ref=grad_s.at[h, pl.ds(start, rows_here)],
            dst_ref=landed.at[h, source],
            send_sem=p_send.at[h, peer],
            recv_sem=p_recv.at[h, source],
            device_id=(peer, d),
            device_id_type=MESH,
        )

    def own_grad(h):
        start = pl.multiple_of(s * rows_here, rows_here)
        return pltpu.make_async_copy(
            grad_s.at[h, pl.ds(start, rows_here)], landed.at[h, s], local_sem.at[2 + h]
        )

    def direct(step):
        return pltpu.make_async_remote_copy(
            src_ref=total_s,
            dst_ref=spread.at[s],
            send_sem=t_send.at[step],
            recv_sem=t_recv.at[s],
            device_id=(lax.rem(s + 2 * step, seq), d),
            device_id_type=MESH,
        )

    def forward(step):
        source = lax.rem(s + seq - 2 * step, seq)
        return pltpu.make_async_remote_copy(
            src_ref=total_s if step == 0 else spread.at[source],
            dst_ref=spread.at[source],
            send_sem=f_send.at[step],
            recv_sem=t_recv.at[source],
            device_id=(partner, d),
            device_id_type=MESH,
        )

    def arrived(source):
        pltpu.make_async_remote_copy(
            src_ref=total_s,
            dst_ref=spread.at[source],
            send_sem=f_send.at[0],
            recv_sem=t_recv.at[source],
            device_id=(partner, d),
            device_id_type=MESH,
        ).wait_recv()

    own_part = pltpu.make_async_copy(dw_s.at[s], parts.at[slot], local_sem.at[0])
    own_total = pltpu.make_async_copy(total_s, spread.at[s], local_sem.at[1])

    barrier = pltpu.get_barrier_semaphore()
    for step in range(1, seq):
        pl.semaphore_signal(barrier, inc=1, device_id=(lax.rem(s + step, seq), d), device_id_type=MESH)
    for row in range(dp):
        for column in range(ratio):
            @pl.when(jnp.logical_or(row != d, d * ratio + column != s))
            def _():
                pl.semaphore_signal(
                    barrier, inc=1, device_id=(d * ratio + column, row), device_id_type=MESH
                )

    pieces = dw_s.shape[0]
    piece = dw_s.shape[1]
    d_weight = lax.dot_general(
        pack_ref[:, 3 * width : 4 * width], g_ref[...], FIRST, preferred_element_type=jnp.float32
    )
    for index in range(pieces):
        dw_s[index] = (d_weight[index * piece : (index + 1) * piece, :] * factor).astype(
            jnp.bfloat16
        )

    @pl.when(home == d)
    def _():
        pl.semaphore_wait(barrier, 2 * seq - 2)

    @pl.when(home != d)
    def _():
        pl.semaphore_wait(barrier, 2 * seq - 1)

    for step in range(seq):
        peer = lax.rem(s + step, seq)

        @pl.when(jnp.logical_or(home != d, peer != s))
        def _():
            w_copy(peer).start()

    @pl.when(home == d)
    def _():
        own_part.start()

    @pl.loop(0, patches // block_rows)
    def _(block):
        rows = pl.ds(pl.multiple_of(block * block_rows, block_rows), block_rows)
        d_out = lax.dot_general(
            g_ref[rows, :], w_ref[...], LAST, preferred_element_type=jnp.float32
        ).astype(jnp.bfloat16)
        for h in range(heads):
            low = h * HEAD_DIM
            q_s[h, rows, :] = pack_ref[rows, low : low + HEAD_DIM]
            k_s[h, rows, :] = pack_ref[rows, width + low : width + low + HEAD_DIM]
            v_s[h, rows, :] = pack_ref[rows, 2 * width + low : 2 * width + low + HEAD_DIM]
            a_h = pack_ref[rows, 3 * width + low : 3 * width + low + HEAD_DIM]
            do_h = d_out[:, low : low + HEAD_DIM]
            do_s[h, rows, :] = do_h
            product = do_h.astype(jnp.float32) * a_h.astype(jnp.float32)
            delta_s[h, block] = jnp.sum(product.T, axis=0, keepdims=True)

    for h in range(heads):
        dk_s[...] = jnp.zeros_like(dk_s)
        dv_s[...] = jnp.zeros_like(dv_s)

        @pl.loop(0, patches // block_rows)
        def _(block):
            rows = pl.ds(pl.multiple_of(block * block_rows, block_rows), block_rows)
            q_b = q_s[h, rows, :]
            do_b = do_s[h, rows, :]
            keys = k_s[h]
            scores = lax.dot_general(keys, q_b, LAST, preferred_element_type=jnp.float32)
            top = jnp.max(scores, axis=0, keepdims=True)
            exps = jnp.exp2((scores - top) * to_log2)
            probs = exps * (1.0 / jnp.sum(exps, axis=0, keepdims=True))
            d_probs = lax.dot_general(v_s[h], do_b, LAST, preferred_element_type=jnp.float32)
            d_scores = (probs * (d_probs - delta_s[h, block]) * scale).astype(jnp.bfloat16)
            dv_s[...] += jnp.dot(probs.astype(jnp.bfloat16), do_b, preferred_element_type=jnp.float32)
            dk_s[...] += jnp.dot(d_scores, q_b, preferred_element_type=jnp.float32)
            dq_t = lax.dot_general(keys, d_scores, FIRST, preferred_element_type=jnp.float32)
            grad_s[h, rows, 0:HEAD_DIM] = dq_t.T.astype(jnp.bfloat16)

        grad_s[h, :, HEAD_DIM : 2 * HEAD_DIM] = dk_s[...].astype(jnp.bfloat16)
        grad_s[h, :, 2 * HEAD_DIM : 3 * HEAD_DIM] = dv_s[...].astype(jnp.bfloat16)

        if h == 0:
            for row in range(dp):
                for column in range(ratio):
                    source = row * ratio + column

                    @pl.when(jnp.logical_or(row != d, d * ratio + column != s))
                    def _():
                        pltpu.make_async_remote_copy(
                            src_ref=dw_s.at[0],
                            dst_ref=parts.at[source],
                            send_sem=w_send.at[0],
                            recv_sem=w_recv.at[source],
                            device_id=(d * ratio + column, row),
                            device_id_type=MESH,
                        ).wait_recv()

            @pl.when(home == d)
            def _():
                own_part.wait()

            for column in range(ratio):
                value = parts[column].astype(jnp.float32)
                for row in range(1, dp):
                    value = value + parts[row * ratio + column].astype(jnp.float32)
                total_s[column] = value.astype(jnp.bfloat16)

        for step in range(1, seq):
            grad_copy(h, lax.rem(s + step, seq), s).start()
        own_grad(h).start()
        if h == 0:
            for step in range(1, seq // 2):
                direct(step).start()
            forward(0).start()
            own_total.start()

    for step in range(1, seq // 2):
        arrived(lax.rem(s + seq - 2 * step, seq))
        forward(step).start()
    for h in range(heads):
        own_grad(h).wait()
        for step in range(1, seq):
            source = lax.rem(s + seq - step, seq)
            grad_copy(h, source, source).wait_recv()
    for step in range(seq // 2):
        arrived(lax.rem(partner + seq - 2 * step, seq))

    own_total.wait()
    for step in range(seq):
        peer = lax.rem(s + step, seq)

        @pl.when(jnp.logical_or(home != d, peer != s))
        def _():
            w_copy(peer).wait_send()

    for step in range(1, seq):
        for h in range(heads):
            grad_copy(h, lax.rem(s + step, seq), s).wait_send()
    for step in range(1, seq // 2):
        direct(step).wait_send()
    for step in range(seq // 2):
        forward(step).wait_send()


def backward(seq, dp, factor, packed, grad_y, w_rows):
    total = packed.shape[0]
    width, features = w_rows.shape
    heads = width // HEAD_DIM
    ratio = seq // dp
    piece = width // seq
    block_rows = 512
    while total % block_rows:
        block_rows //= 2
    dma = pltpu.SemaphoreType.DMA
    vmem = pl.BlockSpec(memory_space=pltpu.VMEM)
    hbm = pl.BlockSpec(memory_space=pl.ANY)
    low = pltpu.VMEM((heads, total, HEAD_DIM), jnp.bfloat16)
    wide = pltpu.VMEM((total, HEAD_DIM), jnp.float32)
    return pl.pallas_call(
        functools.partial(backward_kernel, seq, dp, heads, block_rows, factor),
        out_shape=(
            jax.ShapeDtypeStruct((heads, seq, total // seq, 3 * HEAD_DIM), jnp.bfloat16),
            jax.ShapeDtypeStruct((seq, ratio, piece, features), jnp.bfloat16),
        ),
        in_specs=[vmem] * 3,
        out_specs=(hbm, hbm),
        scratch_shapes=[
            low, low, low, low,
            pltpu.VMEM((heads, total // block_rows, 1, block_rows), jnp.float32),
            wide, wide,
            pltpu.VMEM((heads, total, 3 * HEAD_DIM), jnp.bfloat16),
            pltpu.VMEM((seq, piece, features), jnp.bfloat16),
            pltpu.VMEM((dp * ratio, piece, features), jnp.bfloat16),
            pltpu.VMEM((ratio, piece, features), jnp.bfloat16),
            dma((heads, seq)),
            dma((heads, seq)),
            dma((seq,)),
            dma((dp * ratio,)),
            dma((seq,)),
            dma((seq,)),
            dma((seq,)),
            dma((2 + heads,)),
        ],
        compiler_params=pltpu.CompilerParams(
            collective_id=1, has_side_effects=True, vmem_limit_bytes=VMEM_LIMIT
        ),
        name="attention_backward",
    )(packed, grad_y, w_rows)


def unpack_kernel(landed, spread, dq_ref, dk_ref, dv_ref, out_ref):
    heads, seq = landed.shape[:2]
    ratio, piece = spread.shape[1:3]
    width = heads * HEAD_DIM
    for source in range(seq):
        for h in range(heads):
            start = source * width + h * HEAD_DIM
            for index, ref in enumerate((dq_ref, dk_ref, dv_ref)):
                ref[:, start : start + HEAD_DIM] = landed[
                    h, source, :, index * HEAD_DIM : (index + 1) * HEAD_DIM
                ]
        for column in range(ratio):
            start = column * width + source * piece
            out_ref[start : start + piece, :] = spread[source, column].astype(jnp.float32)


def unpack(dp, landed, spread):
    rows = landed.shape[2]
    features = spread.shape[-1]
    vmem = pl.BlockSpec(memory_space=pltpu.VMEM)
    block = jax.ShapeDtypeStruct((rows, features), jnp.bfloat16)
    return pl.pallas_call(
        unpack_kernel,
        out_shape=(
            block, block, block,
            jax.ShapeDtypeStruct((features // dp, features), jnp.float32),
        ),
        in_specs=[vmem] * 2,
        out_specs=(vmem,) * 4,
        compiler_params=pltpu.CompilerParams(vmem_limit_bytes=VMEM_LIMIT),
        name="unpack",
    )(landed, spread)


def body(query, keys, values, attn, d_block, w_out):
    seq = lax.axis_size("seq")
    dp = lax.axis_size("dp")
    rows, features = query.shape[1:]
    width = features // seq
    flat = lambda array: array.reshape(rows, features)
    packed, grad_y, w_rows = gather(
        seq, dp, flat(query), flat(keys), flat(values), flat(attn), flat(d_block),
        w_out.reshape(seq // dp, width, features),
    )
    factor = 1.0 / float(dp * rows * seq) ** 0.5
    landed, spread = backward(
        seq, dp, factor,
        packed.reshape(seq * rows, 4 * width),
        grad_y.reshape(seq * rows, features),
        w_rows,
    )
    d_query, d_keys, d_values, d_weight = unpack(dp, landed, spread)
    whole = lambda array: array.reshape(1, rows, features)
    return whole(d_query), whole(d_keys), whole(d_values), d_weight


def solution(mesh):
    blocks = P("dp", "seq", None)
    return jax.shard_map(
        body,
        mesh=mesh,
        in_specs=(blocks,) * 5 + (P("dp", None),),
        out_specs=(blocks, blocks, blocks, P("dp", None)),
        check_vma=False,
    )
```

```python
import functools
import math

import jax
import jax.numpy as jnp
from jax import lax
from jax.experimental import pallas as pl
from jax.experimental.pallas import tpu as pltpu
from jax.sharding import PartitionSpec as P

HEAD_DIM = 80
LANES = 128
MESH = pl.DeviceIdType.MESH
VMEM_LIMIT = 60 * 1024 * 1024
LAST = (((1,), (1,)), ((), ()))
FIRST = (((0,), (0,)), ((), ()))


def gather_kernel(
    seq, dp, q_ref, k_ref, v_ref, a_ref, g_ref, w_ref, pack_out, g_out, w_out,
    packed, g_send, g_recv, f_send, w_send, w_recv, p_send, p_recv, local_sem,
):
    s = lax.axis_index("seq")
    d = lax.axis_index("dp")
    ratio = seq // dp
    home = s // ratio
    partner = s + 1 - 2 * (s % 2)
    width = k_ref.shape[1] // seq

    barrier = pltpu.get_barrier_semaphore()
    for step in range(1, seq):
        pl.semaphore_signal(barrier, inc=1, device_id=(lax.rem(s + step, seq), d), device_id_type=MESH)
    for step in range(1, dp):
        pl.semaphore_signal(barrier, inc=1, device_id=(s, lax.rem(d + step, dp)), device_id_type=MESH)
    pl.semaphore_wait(barrier, seq + dp - 2)

    def w_copy(step):
        return pltpu.make_async_remote_copy(
            src_ref=w_ref.at[s % ratio],
            dst_ref=w_out,
            send_sem=w_send.at[step],
            recv_sem=w_recv,
            device_id=(s, lax.rem(d + step, dp)),
            device_id_type=MESH,
        )

    def direct(step):
        return pltpu.make_async_remote_copy(
            src_ref=g_ref,
            dst_ref=g_out.at[s],
            send_sem=g_send.at[step],
            recv_sem=g_recv.at[s],
            device_id=(lax.rem(s + 2 * step, seq), d),
            device_id_type=MESH,
        )

    def forward(step):
        source = lax.rem(s + seq - 2 * step, seq)
        return pltpu.make_async_remote_copy(
            src_ref=g_ref if step == 0 else g_out.at[source],
            dst_ref=g_out.at[source],
            send_sem=f_send.at[step],
            recv_sem=g_recv.at[source],
            device_id=(partner, d),
            device_id_type=MESH,
        )

    def arrived(source):
        pltpu.make_async_remote_copy(
            src_ref=g_ref,
            dst_ref=g_out.at[source],
            send_sem=f_send.at[0],
            recv_sem=g_recv.at[source],
            device_id=(partner, d),
            device_id_type=MESH,
        ).wait_recv()

    def pack_copy(step):
        peer = lax.rem(s + step, seq)
        return pltpu.make_async_remote_copy(
            src_ref=packed.at[peer],
            dst_ref=pack_out.at[s],
            send_sem=p_send.at[step],
            recv_sem=p_recv.at[s],
            device_id=(peer, d),
            device_id_type=MESH,
        )

    own_g = pltpu.make_async_copy(g_ref, g_out.at[s], local_sem.at[0])
    own_w = pltpu.make_async_copy(w_ref.at[s % ratio], w_out, local_sem.at[1])
    own_pack = pltpu.make_async_copy(packed.at[s], pack_out.at[s], local_sem.at[2])

    for step in range(1, seq // 2):
        direct(step).start()
    forward(0).start()
    own_g.start()

    @pl.when(home == d)
    def _():
        for step in range(1, dp):
            w_copy(step).start()
        own_w.start()

    for peer in range(seq):
        for index, ref in enumerate((q_ref, k_ref, v_ref, a_ref)):
            packed[peer, :, index * width : (index + 1) * width] = ref[
                :, peer * width : (peer + 1) * width
            ]
    for step in range(1, seq):
        pack_copy(step).start()
    own_pack.start()

    for step in range(1, seq // 2):
        arrived(lax.rem(s + seq - 2 * step, seq))
        forward(step).start()
    for step in range(seq // 2):
        arrived(lax.rem(partner + seq - 2 * step, seq))
    for step in range(1, seq):
        source = lax.rem(s + seq - step, seq)
        pltpu.make_async_remote_copy(
            src_ref=packed.at[source],
            dst_ref=pack_out.at[source],
            send_sem=p_send.at[step],
            recv_sem=p_recv.at[source],
            device_id=(source, d),
            device_id_type=MESH,
        ).wait_recv()

    @pl.when(home == d)
    def _():
        for step in range(1, dp):
            w_copy(step).wait_send()
        own_w.wait()

    @pl.when(home != d)
    def _():
        w_copy(1).wait_recv()

    own_g.wait()
    own_pack.wait()
    for step in range(1, seq // 2):
        direct(step).wait_send()
    for step in range(seq // 2):
        forward(step).wait_send()
    for step in range(1, seq):
        pack_copy(step).wait_send()


def gather(seq, dp, query, keys, values, attn, grad_y, w_rows):
    rows, features = query.shape
    width = features // seq
    dma = pltpu.SemaphoreType.DMA
    vmem = pl.BlockSpec(memory_space=pltpu.VMEM)
    hbm = pl.BlockSpec(memory_space=pl.ANY)
    return pl.pallas_call(
        functools.partial(gather_kernel, seq, dp),
        out_shape=(
            jax.ShapeDtypeStruct((seq, rows, 4 * width), jnp.bfloat16),
            jax.ShapeDtypeStruct((seq, rows, features), jnp.bfloat16),
            jax.ShapeDtypeStruct((width, features), jnp.bfloat16),
        ),
        in_specs=[vmem] * 6,
        out_specs=(hbm, hbm, hbm),
        scratch_shapes=[
            pltpu.VMEM((seq, rows, 4 * width), jnp.bfloat16),
            dma((seq,)),
            dma((seq,)),
            dma((seq,)),
            dma((dp,)),
            dma(()),
            dma((seq,)),
            dma((seq,)),
            dma((3,)),
        ],
        compiler_params=pltpu.CompilerParams(
            collective_id=0, has_side_effects=True, vmem_limit_bytes=VMEM_LIMIT
        ),
        name="gather_heads",
    )(query, keys, values, attn, grad_y, w_rows)


def backward_kernel(
    seq, dp, heads, block_rows, factor, pack_ref, g_ref, w_ref, landed, spread,
    q_s, k_s, v_s, do_s, delta_s, dk_s, dv_s, grad_s, dw_s, middle, parts, total_s,
    p_send, p_recv, w_send, w_recv, z_send, z_recv, t_send, f_send, t_recv, local_sem,
):
    s = lax.axis_index("seq")
    d = lax.axis_index("dp")
    ratio = seq // dp
    partner = s + 1 - 2 * (s % 2)
    patches = pack_ref.shape[0]
    rows_here = patches // seq
    width = heads * HEAD_DIM
    scale = HEAD_DIM ** (-0.5)
    to_log2 = scale * math.log2(math.e)

    def w_copy(peer, source):
        return pltpu.make_async_remote_copy(
            src_ref=dw_s.at[peer],
            dst_ref=middle.at[source],
            send_sem=w_send.at[peer],
            recv_sem=w_recv.at[source],
            device_id=(peer, d),
            device_id_type=MESH,
        )

    def z_copy(plane, source):
        return pltpu.make_async_remote_copy(
            src_ref=middle.at[pl.ds(plane * ratio, ratio)],
            dst_ref=parts.at[source],
            send_sem=z_send.at[plane],
            recv_sem=z_recv.at[source],
            device_id=(s, plane),
            device_id_type=MESH,
        )

    def grad_copy(h, peer, source):
        start = pl.multiple_of(peer * rows_here, rows_here)
        return pltpu.make_async_remote_copy(
            src_ref=grad_s.at[h, pl.ds(start, rows_here)],
            dst_ref=landed.at[h, source],
            send_sem=p_send.at[h, peer],
            recv_sem=p_recv.at[h, source],
            device_id=(peer, d),
            device_id_type=MESH,
        )

    def own_grad(h):
        start = pl.multiple_of(s * rows_here, rows_here)
        return pltpu.make_async_copy(
            grad_s.at[h, pl.ds(start, rows_here)], landed.at[h, s], local_sem.at[2 + h]
        )

    def direct(step):
        return pltpu.make_async_remote_copy(
            src_ref=total_s,
            dst_ref=spread.at[s],
            send_sem=t_send.at[step],
            recv_sem=t_recv.at[s],
            device_id=(lax.rem(s + 2 * step, seq), d),
            device_id_type=MESH,
        )

    def forward(step):
        source = lax.rem(s + seq - 2 * step, seq)
        return pltpu.make_async_remote_copy(
            src_ref=total_s if step == 0 else spread.at[source],
            dst_ref=spread.at[source],
            send_sem=f_send.at[step],
            recv_sem=t_recv.at[source],
            device_id=(partner, d),
            device_id_type=MESH,
        )

    def arrived(source):
        pltpu.make_async_remote_copy(
            src_ref=total_s,
            dst_ref=spread.at[source],
            send_sem=f_send.at[0],
            recv_sem=t_recv.at[source],
            device_id=(partner, d),
            device_id_type=MESH,
        ).wait_recv()

    own_middle = pltpu.make_async_copy(dw_s.at[s], middle.at[s], local_sem.at[0])
    own_part = pltpu.make_async_copy(
        middle.at[pl.ds(d * ratio, ratio)], parts.at[d], local_sem.at[2 + heads]
    )
    own_total = pltpu.make_async_copy(total_s, spread.at[s], local_sem.at[1])

    barrier = pltpu.get_barrier_semaphore()
    for step in range(1, seq):
        pl.semaphore_signal(barrier, inc=1, device_id=(lax.rem(s + step, seq), d), device_id_type=MESH)
    for step in range(1, dp):
        pl.semaphore_signal(barrier, inc=1, device_id=(s, lax.rem(d + step, dp)), device_id_type=MESH)

    piece = width // seq
    groups = g_ref.shape[1] // LANES
    used = piece * groups
    d_weight = lax.dot_general(
        pack_ref[:, 3 * width : 4 * width], g_ref[...], FIRST, preferred_element_type=jnp.float32
    )
    d_weight = d_weight * factor
    for index in range(seq):
        share = d_weight[index * piece : (index + 1) * piece, :]
        tall = [share[:, group * LANES : (group + 1) * LANES] for group in range(groups)]
        tall.append(jnp.zeros((dw_s.shape[1] - used, LANES), jnp.float32))
        dw_s[index] = jnp.concatenate(tall, axis=0).astype(jnp.bfloat16)

    pl.semaphore_wait(barrier, seq + dp - 2)
    for step in range(1, seq):
        w_copy(lax.rem(s + step, seq), s).start()
    own_middle.start()

    def relay():
        own_middle.wait()
        for step in range(1, seq):
            source = lax.rem(s + seq - step, seq)
            w_copy(source, source).wait_recv()
        for step in range(1, dp):
            z_copy(lax.rem(d + step, dp), d).start()
        own_part.start()

    def combine():
        own_part.wait()
        for step in range(1, dp):
            source = lax.rem(d + dp - step, dp)
            z_copy(source, source).wait_recv()
        for column in range(ratio):
            value = parts[0, column].astype(jnp.float32)
            for plane in range(1, dp):
                value = value + parts[plane, column].astype(jnp.float32)
            total_s[column] = value.astype(jnp.bfloat16)
        for step in range(1, seq // 2):
            direct(step).start()
        forward(0).start()
        own_total.start()

    @pl.loop(0, patches // block_rows)
    def _(block):
        rows = pl.ds(pl.multiple_of(block * block_rows, block_rows), block_rows)
        d_out = lax.dot_general(
            g_ref[rows, :], w_ref[...], LAST, preferred_element_type=jnp.float32
        ).astype(jnp.bfloat16)
        for h in range(heads):
            low = h * HEAD_DIM
            q_s[h, rows, :] = pack_ref[rows, low : low + HEAD_DIM]
            k_s[h, rows, :] = pack_ref[rows, width + low : width + low + HEAD_DIM]
            v_s[h, rows, :] = pack_ref[rows, 2 * width + low : 2 * width + low + HEAD_DIM]
            a_h = pack_ref[rows, 3 * width + low : 3 * width + low + HEAD_DIM]
            do_h = d_out[:, low : low + HEAD_DIM]
            do_s[h, rows, :] = do_h
            product = do_h.astype(jnp.float32) * a_h.astype(jnp.float32)
            delta_s[h, block] = jnp.sum(product.T, axis=0, keepdims=True)

    blocks = patches // block_rows
    for h in range(heads):
        dk_s[...] = jnp.zeros_like(dk_s)
        dv_s[...] = jnp.zeros_like(dv_s)

        @pl.loop(0, patches // block_rows)
        def _(block):
            rows = pl.ds(pl.multiple_of(block * block_rows, block_rows), block_rows)
            if h == 0:
                pl.when(block == min(1, blocks - 1))(relay)
            if h == heads - 1:
                pl.when(block == min(1 if heads > 1 else 2, blocks - 1))(combine)
            q_b = q_s[h, rows, :]
            do_b = do_s[h, rows, :]
            keys = k_s[h]
            scores = lax.dot_general(keys, q_b, LAST, preferred_element_type=jnp.float32)
            top = jnp.max(scores, axis=0, keepdims=True)
            exps = jnp.exp2((scores - top) * to_log2)
            probs = exps * (1.0 / jnp.sum(exps, axis=0, keepdims=True))
            d_probs = lax.dot_general(v_s[h], do_b, LAST, preferred_element_type=jnp.float32)
            d_scores = (probs * (d_probs - delta_s[h, block]) * scale).astype(jnp.bfloat16)
            dv_s[...] += jnp.dot(probs.astype(jnp.bfloat16), do_b, preferred_element_type=jnp.float32)
            dk_s[...] += jnp.dot(d_scores, q_b, preferred_element_type=jnp.float32)
            dq_t = lax.dot_general(keys, d_scores, FIRST, preferred_element_type=jnp.float32)
            grad_s[h, rows, 0:HEAD_DIM] = dq_t.T.astype(jnp.bfloat16)

        grad_s[h, :, HEAD_DIM : 2 * HEAD_DIM] = dk_s[...].astype(jnp.bfloat16)
        grad_s[h, :, 2 * HEAD_DIM : 3 * HEAD_DIM] = dv_s[...].astype(jnp.bfloat16)

        for step in range(1, seq):
            grad_copy(h, lax.rem(s + step, seq), s).start()
        own_grad(h).start()

    for step in range(1, seq // 2):
        arrived(lax.rem(s + seq - 2 * step, seq))
        forward(step).start()
    for h in range(heads):
        own_grad(h).wait()
        for step in range(1, seq):
            source = lax.rem(s + seq - step, seq)
            grad_copy(h, source, source).wait_recv()
    for step in range(seq // 2):
        arrived(lax.rem(partner + seq - 2 * step, seq))

    own_total.wait()
    for step in range(1, seq):
        w_copy(lax.rem(s + step, seq), s).wait_send()
    for step in range(1, dp):
        z_copy(lax.rem(d + step, dp), d).wait_send()

    for step in range(1, seq):
        for h in range(heads):
            grad_copy(h, lax.rem(s + step, seq), s).wait_send()
    for step in range(1, seq // 2):
        direct(step).wait_send()
    for step in range(seq // 2):
        forward(step).wait_send()


def backward(seq, dp, factor, packed, grad_y, w_rows):
    total = packed.shape[0]
    width, features = w_rows.shape
    heads = width // HEAD_DIM
    ratio = seq // dp
    tall = -(-(width // seq * features // LANES) // 16) * 16
    block_rows = 512
    while total % block_rows:
        block_rows //= 2
    dma = pltpu.SemaphoreType.DMA
    vmem = pl.BlockSpec(memory_space=pltpu.VMEM)
    hbm = pl.BlockSpec(memory_space=pl.ANY)
    low = pltpu.VMEM((heads, total, HEAD_DIM), jnp.bfloat16)
    wide = pltpu.VMEM((total, HEAD_DIM), jnp.float32)
    return pl.pallas_call(
        functools.partial(backward_kernel, seq, dp, heads, block_rows, factor),
        out_shape=(
            jax.ShapeDtypeStruct((heads, seq, total // seq, 3 * HEAD_DIM), jnp.bfloat16),
            jax.ShapeDtypeStruct((seq, ratio, tall, LANES), jnp.bfloat16),
        ),
        in_specs=[vmem] * 3,
        out_specs=(hbm, hbm),
        scratch_shapes=[
            low, low, low, low,
            pltpu.VMEM((heads, total // block_rows, 1, block_rows), jnp.float32),
            wide, wide,
            pltpu.VMEM((heads, total, 3 * HEAD_DIM), jnp.bfloat16),
            pltpu.VMEM((seq, tall, LANES), jnp.bfloat16),
            pltpu.VMEM((seq, tall, LANES), jnp.bfloat16),
            pltpu.VMEM((dp, ratio, tall, LANES), jnp.bfloat16),
            pltpu.VMEM((ratio, tall, LANES), jnp.bfloat16),
            dma((heads, seq)),
            dma((heads, seq)),
            dma((seq,)),
            dma((seq,)),
            dma((dp,)),
            dma((dp,)),
            dma((seq,)),
            dma((seq,)),
            dma((seq,)),
            dma((3 + heads,)),
        ],
        compiler_params=pltpu.CompilerParams(
            collective_id=1, has_side_effects=True, vmem_limit_bytes=VMEM_LIMIT
        ),
        name="attention_backward",
    )(packed, grad_y, w_rows)


def unpack_kernel(landed, spread, dq_ref, dk_ref, dv_ref, out_ref):
    heads, seq = landed.shape[:2]
    ratio = spread.shape[1]
    width = heads * HEAD_DIM
    piece = width // seq
    groups = out_ref.shape[1] // LANES
    for source in range(seq):
        for h in range(heads):
            start = source * width + h * HEAD_DIM
            for index, ref in enumerate((dq_ref, dk_ref, dv_ref)):
                ref[:, start : start + HEAD_DIM] = landed[
                    h, source, :, index * HEAD_DIM : (index + 1) * HEAD_DIM
                ]
        for column in range(ratio):
            start = column * width + source * piece
            tall = spread[source, column].astype(jnp.float32)
            for group in range(groups):
                out_ref[start : start + piece, group * LANES : (group + 1) * LANES] = tall[
                    group * piece : (group + 1) * piece
                ]


def unpack(dp, landed, spread):
    rows = landed.shape[2]
    features = landed.shape[0] * landed.shape[1] * HEAD_DIM
    vmem = pl.BlockSpec(memory_space=pltpu.VMEM)
    block = jax.ShapeDtypeStruct((rows, features), jnp.bfloat16)
    return pl.pallas_call(
        unpack_kernel,
        out_shape=(
            block, block, block,
            jax.ShapeDtypeStruct((features // dp, features), jnp.float32),
        ),
        in_specs=[vmem] * 2,
        out_specs=(vmem,) * 4,
        compiler_params=pltpu.CompilerParams(vmem_limit_bytes=VMEM_LIMIT),
        name="unpack",
    )(landed, spread)


def body(query, keys, values, attn, d_block, w_out):
    seq = lax.axis_size("seq")
    dp = lax.axis_size("dp")
    rows, features = query.shape[1:]
    width = features // seq
    flat = lambda array: array.reshape(rows, features)
    packed, grad_y, w_rows = gather(
        seq, dp, flat(query), flat(keys), flat(values), flat(attn), flat(d_block),
        w_out.reshape(seq // dp, width, features),
    )
    factor = 1.0 / float(dp * rows * seq) ** 0.5
    landed, spread = backward(
        seq, dp, factor,
        packed.reshape(seq * rows, 4 * width),
        grad_y.reshape(seq * rows, features),
        w_rows,
    )
    d_query, d_keys, d_values, d_weight = unpack(dp, landed, spread)
    whole = lambda array: array.reshape(1, rows, features)
    return whole(d_query), whole(d_keys), whole(d_values), d_weight


def solution(mesh):
    blocks = P("dp", "seq", None)
    return jax.shard_map(
        body,
        mesh=mesh,
        in_specs=(blocks,) * 5 + (P("dp", None),),
        out_specs=(blocks, blocks, blocks, P("dp", None)),
        check_vma=False,
    )
```

```python
import functools
import math

import jax
import jax.numpy as jnp
from jax import lax
from jax.experimental import pallas as pl
from jax.experimental.pallas import tpu as pltpu
from jax.sharding import PartitionSpec as P

HEAD_DIM = 80
LANES = 128
MESH = pl.DeviceIdType.MESH
VMEM_LIMIT = 60 * 1024 * 1024
LAST = (((1,), (1,)), ((), ()))
FIRST = (((0,), (0,)), ((), ()))


def gather_kernel(
    seq, dp, q_ref, k_ref, v_ref, a_ref, g_ref, w_ref, pack_out, g_out, w_out,
    packed, g_send, g_recv, f_send, w_send, w_recv, p_send, p_recv, local_sem,
):
    s = lax.axis_index("seq")
    d = lax.axis_index("dp")
    ratio = seq // dp
    home = s // ratio
    partner = s + 1 - 2 * (s % 2)
    width = k_ref.shape[1] // seq

    barrier = pltpu.get_barrier_semaphore()
    for step in range(1, seq):
        pl.semaphore_signal(barrier, inc=1, device_id=(lax.rem(s + step, seq), d), device_id_type=MESH)
    for step in range(1, dp):
        pl.semaphore_signal(barrier, inc=1, device_id=(s, lax.rem(d + step, dp)), device_id_type=MESH)
    pl.semaphore_wait(barrier, seq + dp - 2)

    def w_copy(step):
        return pltpu.make_async_remote_copy(
            src_ref=w_ref.at[s % ratio],
            dst_ref=w_out,
            send_sem=w_send.at[step],
            recv_sem=w_recv,
            device_id=(s, lax.rem(d + step, dp)),
            device_id_type=MESH,
        )

    def direct(step):
        return pltpu.make_async_remote_copy(
            src_ref=g_ref,
            dst_ref=g_out.at[s],
            send_sem=g_send.at[step],
            recv_sem=g_recv.at[s],
            device_id=(lax.rem(s + 2 * step, seq), d),
            device_id_type=MESH,
        )

    def forward(step):
        source = lax.rem(s + seq - 2 * step, seq)
        return pltpu.make_async_remote_copy(
            src_ref=g_ref if step == 0 else g_out.at[source],
            dst_ref=g_out.at[source],
            send_sem=f_send.at[step],
            recv_sem=g_recv.at[source],
            device_id=(partner, d),
            device_id_type=MESH,
        )

    def arrived(source):
        pltpu.make_async_remote_copy(
            src_ref=g_ref,
            dst_ref=g_out.at[source],
            send_sem=f_send.at[0],
            recv_sem=g_recv.at[source],
            device_id=(partner, d),
            device_id_type=MESH,
        ).wait_recv()

    def pack_copy(step):
        peer = lax.rem(s + step, seq)
        return pltpu.make_async_remote_copy(
            src_ref=packed.at[peer],
            dst_ref=pack_out.at[s],
            send_sem=p_send.at[step],
            recv_sem=p_recv.at[s],
            device_id=(peer, d),
            device_id_type=MESH,
        )

    own_g = pltpu.make_async_copy(g_ref, g_out.at[s], local_sem.at[0])
    own_w = pltpu.make_async_copy(w_ref.at[s % ratio], w_out, local_sem.at[1])
    own_pack = pltpu.make_async_copy(packed.at[s], pack_out.at[s], local_sem.at[2])

    for step in range(1, seq // 2):
        direct(step).start()
    forward(0).start()
    own_g.start()

    @pl.when(home == d)
    def _():
        for step in range(1, dp):
            w_copy(step).start()
        own_w.start()

    for peer in range(seq):
        for index, ref in enumerate((q_ref, k_ref, v_ref, a_ref)):
            packed[peer, :, index * width : (index + 1) * width] = ref[
                :, peer * width : (peer + 1) * width
            ]
    for step in range(1, seq):
        pack_copy(step).start()
    own_pack.start()

    for step in range(1, seq // 2):
        arrived(lax.rem(s + seq - 2 * step, seq))
        forward(step).start()
    for step in range(seq // 2):
        arrived(lax.rem(partner + seq - 2 * step, seq))
    for step in range(1, seq):
        source = lax.rem(s + seq - step, seq)
        pltpu.make_async_remote_copy(
            src_ref=packed.at[source],
            dst_ref=pack_out.at[source],
            send_sem=p_send.at[step],
            recv_sem=p_recv.at[source],
            device_id=(source, d),
            device_id_type=MESH,
        ).wait_recv()

    @pl.when(home == d)
    def _():
        for step in range(1, dp):
            w_copy(step).wait_send()
        own_w.wait()

    @pl.when(home != d)
    def _():
        w_copy(1).wait_recv()

    own_g.wait()
    own_pack.wait()
    for step in range(1, seq // 2):
        direct(step).wait_send()
    for step in range(seq // 2):
        forward(step).wait_send()
    for step in range(1, seq):
        pack_copy(step).wait_send()


def gather(seq, dp, query, keys, values, attn, grad_y, w_rows):
    rows, features = query.shape
    width = features // seq
    dma = pltpu.SemaphoreType.DMA
    vmem = pl.BlockSpec(memory_space=pltpu.VMEM)
    hbm = pl.BlockSpec(memory_space=pl.ANY)
    return pl.pallas_call(
        functools.partial(gather_kernel, seq, dp),
        out_shape=(
            jax.ShapeDtypeStruct((seq, rows, 4 * width), jnp.bfloat16),
            jax.ShapeDtypeStruct((seq, rows, features), jnp.bfloat16),
            jax.ShapeDtypeStruct((width, features), jnp.bfloat16),
        ),
        in_specs=[vmem] * 6,
        out_specs=(hbm, hbm, hbm),
        scratch_shapes=[
            pltpu.VMEM((seq, rows, 4 * width), jnp.bfloat16),
            dma((seq,)),
            dma((seq,)),
            dma((seq,)),
            dma((dp,)),
            dma(()),
            dma((seq,)),
            dma((seq,)),
            dma((3,)),
        ],
        compiler_params=pltpu.CompilerParams(
            collective_id=0, has_side_effects=True, vmem_limit_bytes=VMEM_LIMIT
        ),
        name="gather_heads",
    )(query, keys, values, attn, grad_y, w_rows)


def backward_kernel(
    seq, dp, heads, block_rows, factor, pack_ref, g_ref, w_ref, landed, spread,
    q_s, k_s, v_s, do_s, delta_s, dk_s, dv_s, grad_s, dw_s, middle, parts, total_s,
    p_send, p_recv, w_send, w_recv, z_send, z_recv, t_send, f_send, t_recv, local_sem,
):
    s = lax.axis_index("seq")
    d = lax.axis_index("dp")
    ratio = seq // dp
    partner = s + 1 - 2 * (s % 2)
    patches = pack_ref.shape[0]
    rows_here = patches // seq
    width = heads * HEAD_DIM
    scale = HEAD_DIM ** (-0.5)
    to_log2 = scale * math.log2(math.e)

    def w_copy(peer, source):
        return pltpu.make_async_remote_copy(
            src_ref=dw_s.at[peer],
            dst_ref=middle.at[source],
            send_sem=w_send.at[peer],
            recv_sem=w_recv.at[source],
            device_id=(peer, d),
            device_id_type=MESH,
        )

    def z_copy(plane, source):
        return pltpu.make_async_remote_copy(
            src_ref=middle.at[pl.ds(plane * ratio, ratio)],
            dst_ref=parts.at[source],
            send_sem=z_send.at[plane],
            recv_sem=z_recv.at[source],
            device_id=(s, plane),
            device_id_type=MESH,
        )

    def grad_copy(h, peer, source):
        start = pl.multiple_of(peer * rows_here, rows_here)
        return pltpu.make_async_remote_copy(
            src_ref=grad_s.at[h, pl.ds(start, rows_here)],
            dst_ref=landed.at[h, source],
            send_sem=p_send.at[h, peer],
            recv_sem=p_recv.at[h, source],
            device_id=(peer, d),
            device_id_type=MESH,
        )

    def own_grad(h):
        start = pl.multiple_of(s * rows_here, rows_here)
        return pltpu.make_async_copy(
            grad_s.at[h, pl.ds(start, rows_here)], landed.at[h, s], local_sem.at[2 + h]
        )

    def direct(step):
        return pltpu.make_async_remote_copy(
            src_ref=total_s,
            dst_ref=spread.at[s],
            send_sem=t_send.at[step],
            recv_sem=t_recv.at[s],
            device_id=(lax.rem(s + 2 * step, seq), d),
            device_id_type=MESH,
        )

    def forward(step):
        source = lax.rem(s + seq - 2 * step, seq)
        return pltpu.make_async_remote_copy(
            src_ref=total_s if step == 0 else spread.at[source],
            dst_ref=spread.at[source],
            send_sem=f_send.at[step],
            recv_sem=t_recv.at[source],
            device_id=(partner, d),
            device_id_type=MESH,
        )

    def arrived(source):
        pltpu.make_async_remote_copy(
            src_ref=total_s,
            dst_ref=spread.at[source],
            send_sem=f_send.at[0],
            recv_sem=t_recv.at[source],
            device_id=(partner, d),
            device_id_type=MESH,
        ).wait_recv()

    own_middle = pltpu.make_async_copy(dw_s.at[s], middle.at[s], local_sem.at[0])
    own_part = pltpu.make_async_copy(
        middle.at[pl.ds(d * ratio, ratio)], parts.at[d], local_sem.at[2 + heads]
    )
    own_total = pltpu.make_async_copy(total_s, spread.at[s], local_sem.at[1])

    barrier = pltpu.get_barrier_semaphore()
    for step in range(1, seq):
        pl.semaphore_signal(barrier, inc=1, device_id=(lax.rem(s + step, seq), d), device_id_type=MESH)
    for step in range(1, dp):
        pl.semaphore_signal(barrier, inc=1, device_id=(s, lax.rem(d + step, dp)), device_id_type=MESH)

    piece = width // seq
    groups = g_ref.shape[1] // LANES
    used = piece * groups
    d_weight = lax.dot_general(
        pack_ref[:, 3 * width : 4 * width], g_ref[...], FIRST, preferred_element_type=jnp.float32
    )
    d_weight = d_weight * factor
    for index in range(seq):
        share = d_weight[index * piece : (index + 1) * piece, :]
        tall = [share[:, group * LANES : (group + 1) * LANES] for group in range(groups)]
        tall.append(jnp.zeros((dw_s.shape[1] - used, LANES), jnp.float32))
        dw_s[index] = jnp.concatenate(tall, axis=0).astype(jnp.bfloat16)

    pl.semaphore_wait(barrier, seq + dp - 2)
    for step in range(1, seq):
        w_copy(lax.rem(s + step, seq), s).start()
    own_middle.start()

    def relay():
        own_middle.wait()
        for step in range(1, seq):
            source = lax.rem(s + seq - step, seq)
            w_copy(source, source).wait_recv()
        for step in range(1, dp):
            z_copy(lax.rem(d + step, dp), d).start()
        own_part.start()

    def combine():
        own_part.wait()
        for step in range(1, dp):
            source = lax.rem(d + dp - step, dp)
            z_copy(source, source).wait_recv()
        for column in range(ratio):
            value = parts[0, column].astype(jnp.float32)
            for plane in range(1, dp):
                value = value + parts[plane, column].astype(jnp.float32)
            total_s[column] = value.astype(jnp.bfloat16)
        for step in range(1, seq // 2):
            direct(step).start()
        forward(0).start()
        own_total.start()

    @pl.loop(0, patches // block_rows)
    def _(block):
        rows = pl.ds(pl.multiple_of(block * block_rows, block_rows), block_rows)
        d_out = lax.dot_general(
            g_ref[rows, :], w_ref[...], LAST, preferred_element_type=jnp.float32
        ).astype(jnp.bfloat16)
        for h in range(heads):
            low = h * HEAD_DIM
            q_s[h, rows, :] = pack_ref[rows, low : low + HEAD_DIM]
            k_s[h, rows, :] = pack_ref[rows, width + low : width + low + HEAD_DIM]
            v_s[h, rows, :] = pack_ref[rows, 2 * width + low : 2 * width + low + HEAD_DIM]
            a_h = pack_ref[rows, 3 * width + low : 3 * width + low + HEAD_DIM]
            do_h = d_out[:, low : low + HEAD_DIM]
            do_s[h, rows, :] = do_h
            product = do_h.astype(jnp.float32) * a_h.astype(jnp.float32)
            delta_s[h, block] = jnp.sum(product.T, axis=0, keepdims=True)

    blocks = patches // block_rows
    for h in range(heads):
        dk_s[...] = jnp.zeros_like(dk_s)
        dv_s[...] = jnp.zeros_like(dv_s)

        @pl.loop(0, patches // block_rows)
        def _(block):
            rows = pl.ds(pl.multiple_of(block * block_rows, block_rows), block_rows)
            if h == 0:
                pl.when(block == min(1, blocks - 1))(relay)
            if h == heads - 1:
                pl.when(block == min(1 if heads > 1 else 2, blocks - 1))(combine)
            q_b = q_s[h, rows, :]
            do_b = do_s[h, rows, :]
            keys = k_s[h]
            scores = lax.dot_general(keys, q_b, LAST, preferred_element_type=jnp.float32)
            top = jnp.max(scores, axis=0, keepdims=True)
            exps = jnp.exp2((scores - top) * to_log2)
            probs = exps * (1.0 / jnp.sum(exps, axis=0, keepdims=True))
            d_probs = lax.dot_general(v_s[h], do_b, LAST, preferred_element_type=jnp.float32)
            d_scores = (probs * (d_probs - delta_s[h, block]) * scale).astype(jnp.bfloat16)
            dv_s[...] += jnp.dot(probs.astype(jnp.bfloat16), do_b, preferred_element_type=jnp.float32)
            dk_s[...] += jnp.dot(d_scores, q_b, preferred_element_type=jnp.float32)
            dq_t = lax.dot_general(keys, d_scores, FIRST, preferred_element_type=jnp.float32)
            grad_s[h, rows, 0:HEAD_DIM] = dq_t.T.astype(jnp.bfloat16)

        grad_s[h, :, HEAD_DIM : 2 * HEAD_DIM] = dk_s[...].astype(jnp.bfloat16)
        grad_s[h, :, 2 * HEAD_DIM : 3 * HEAD_DIM] = dv_s[...].astype(jnp.bfloat16)

        for step in range(1, seq):
            grad_copy(h, lax.rem(s + step, seq), s).start()
        own_grad(h).start()

    for step in range(1, seq // 2):
        arrived(lax.rem(s + seq - 2 * step, seq))
        forward(step).start()
    for h in range(heads):
        own_grad(h).wait()
        for step in range(1, seq):
            source = lax.rem(s + seq - step, seq)
            grad_copy(h, source, source).wait_recv()
    for step in range(seq // 2):
        arrived(lax.rem(partner + seq - 2 * step, seq))

    own_total.wait()
    for step in range(1, seq):
        w_copy(lax.rem(s + step, seq), s).wait_send()
    for step in range(1, dp):
        z_copy(lax.rem(d + step, dp), d).wait_send()

    for step in range(1, seq):
        for h in range(heads):
            grad_copy(h, lax.rem(s + step, seq), s).wait_send()
    for step in range(1, seq // 2):
        direct(step).wait_send()
    for step in range(seq // 2):
        forward(step).wait_send()


def backward(seq, dp, factor, packed, grad_y, w_rows):
    total = packed.shape[0]
    width, features = w_rows.shape
    heads = width // HEAD_DIM
    ratio = seq // dp
    tall = -(-(width // seq * features // LANES) // 16) * 16
    block_rows = 768
    while total % block_rows:
        block_rows //= 2
    dma = pltpu.SemaphoreType.DMA
    vmem = pl.BlockSpec(memory_space=pltpu.VMEM)
    hbm = pl.BlockSpec(memory_space=pl.ANY)
    low = pltpu.VMEM((heads, total, HEAD_DIM), jnp.bfloat16)
    wide = pltpu.VMEM((total, HEAD_DIM), jnp.float32)
    return pl.pallas_call(
        functools.partial(backward_kernel, seq, dp, heads, block_rows, factor),
        out_shape=(
            jax.ShapeDtypeStruct((heads, seq, total // seq, 3 * HEAD_DIM), jnp.bfloat16),
            jax.ShapeDtypeStruct((seq, ratio, tall, LANES), jnp.bfloat16),
        ),
        in_specs=[vmem] * 3,
        out_specs=(hbm, hbm),
        scratch_shapes=[
            low, low, low, low,
            pltpu.VMEM((heads, total // block_rows, 1, block_rows), jnp.float32),
            wide, wide,
            pltpu.VMEM((heads, total, 3 * HEAD_DIM), jnp.bfloat16),
            pltpu.VMEM((seq, tall, LANES), jnp.bfloat16),
            pltpu.VMEM((seq, tall, LANES), jnp.bfloat16),
            pltpu.VMEM((dp, ratio, tall, LANES), jnp.bfloat16),
            pltpu.VMEM((ratio, tall, LANES), jnp.bfloat16),
            dma((heads, seq)),
            dma((heads, seq)),
            dma((seq,)),
            dma((seq,)),
            dma((dp,)),
            dma((dp,)),
            dma((seq,)),
            dma((seq,)),
            dma((seq,)),
            dma((3 + heads,)),
        ],
        compiler_params=pltpu.CompilerParams(
            collective_id=1, has_side_effects=True, vmem_limit_bytes=VMEM_LIMIT
        ),
        name="attention_backward",
    )(packed, grad_y, w_rows)


def unpack_kernel(landed, spread, dq_ref, dk_ref, dv_ref, out_ref):
    heads, seq = landed.shape[:2]
    ratio = spread.shape[1]
    width = heads * HEAD_DIM
    piece = width // seq
    groups = out_ref.shape[1] // LANES
    for source in range(seq):
        for h in range(heads):
            start = source * width + h * HEAD_DIM
            for index, ref in enumerate((dq_ref, dk_ref, dv_ref)):
                ref[:, start : start + HEAD_DIM] = landed[
                    h, source, :, index * HEAD_DIM : (index + 1) * HEAD_DIM
                ]
        for column in range(ratio):
            start = column * width + source * piece
            tall = spread[source, column].astype(jnp.float32)
            for group in range(groups):
                out_ref[start : start + piece, group * LANES : (group + 1) * LANES] = tall[
                    group * piece : (group + 1) * piece
                ]


def unpack(dp, landed, spread):
    rows = landed.shape[2]
    features = landed.shape[0] * landed.shape[1] * HEAD_DIM
    vmem = pl.BlockSpec(memory_space=pltpu.VMEM)
    block = jax.ShapeDtypeStruct((rows, features), jnp.bfloat16)
    return pl.pallas_call(
        unpack_kernel,
        out_shape=(
            block, block, block,
            jax.ShapeDtypeStruct((features // dp, features), jnp.float32),
        ),
        in_specs=[vmem] * 2,
        out_specs=(vmem,) * 4,
        compiler_params=pltpu.CompilerParams(vmem_limit_bytes=VMEM_LIMIT),
        name="unpack",
    )(landed, spread)


def body(query, keys, values, attn, d_block, w_out):
    seq = lax.axis_size("seq")
    dp = lax.axis_size("dp")
    rows, features = query.shape[1:]
    width = features // seq
    flat = lambda array: array.reshape(rows, features)
    packed, grad_y, w_rows = gather(
        seq, dp, flat(query), flat(keys), flat(values), flat(attn), flat(d_block),
        w_out.reshape(seq // dp, width, features),
    )
    factor = 1.0 / float(dp * rows * seq) ** 0.5
    landed, spread = backward(
        seq, dp, factor,
        packed.reshape(seq * rows, 4 * width),
        grad_y.reshape(seq * rows, features),
        w_rows,
    )
    d_query, d_keys, d_values, d_weight = unpack(dp, landed, spread)
    whole = lambda array: array.reshape(1, rows, features)
    return whole(d_query), whole(d_keys), whole(d_values), d_weight


def solution(mesh):
    blocks = P("dp", "seq", None)
    return jax.shard_map(
        body,
        mesh=mesh,
        in_specs=(blocks,) * 5 + (P("dp", None),),
        out_specs=(blocks, blocks, blocks, P("dp", None)),
        check_vma=False,
    )
```
